512 devices in a mesh: ep: 64 (over x, y, core), hs: 8 (over z).
Axes of the slice: x: 4, y: 8, z: 8, core: 2. Of those that a mesh axis runs over, the one named last changes fastest.
Arguments:
- tokens: bfloat16 [2048, 4096], P('ep'), may hold values from -6 to 6
- expert_ids: int32 [2048, 8], P('ep'), may hold values from 0 to 63, all different within a row; in each aligned block of 32 rows (0 to 31, 32 to 63, ...) at most 8 rows name the same one
- gate_scores: float32 [2048, 8], P('ep'), may hold values from 0.1 to 1
- gate_weight: bfloat16 [64, 4096, 1024], P('ep', None, 'hs'), may hold values from -0.09375 to 0.09375
- up_weight: bfloat16 [64, 4096, 1024], P('ep', None, 'hs'), may hold values from -0.09375 to 0.09375
- down_weight: bfloat16 [64, 1024, 4096], P('ep', 'hs'), may hold values from -0.25 to 0.25
Outputs:
- mixed: bfloat16 [2048, 4096], P('ep', 'hs')
The draws below stay inside these ranges and needn't reach their ends.
Inputs may be any that keep to these rules, and one draw needn't show every extreme that they name: `expert_ids`: each token names 8 different experts; among the 32 tokens of one index of ep no expert is named more than 8 times, a bound that some block reaches.
All inputs are finite; a program needn't handle non-finite values.
Results may differ from the reference program's by a relative error of at most 0.015.
Values may be sent and summed in bfloat16 or wider, within the bound.
A program may use at most 64 MiB of HBM per device.

```python
import math
import jax
import jax.numpy as jnp
import numpy as np
from jax import lax

D = 4096
FF = 1024
TOP = 8
TOK_EP = 32
EXPERTS = 64
CAP = 8
TOKENS = 2048
N_EP = 64
N_HS = 8


def raised(values, stream_key, source, target, shards_of, factor):
    owner, partner = [(jnp.arange(values.shape[dim]) // (values.shape[dim] // shards_of)).reshape([-1 if axis == dim else 1 for axis in range(values.ndim)]) for dim in (source, target)]
    chosen = jax.random.permutation(stream_key, shards_of)[partner]
    strong = (owner == chosen) | (owner == (partner + shards_of // 2) % shards_of)
    return jnp.where(strong, factor * values, values)


def level_of(key, dims, pieces, smallest, top_value):
    gain, own = 1.0, jax.random.fold_in(key, 6)
    for dim, parts in pieces:
        draws = jnp.exp(jax.random.uniform(jax.random.fold_in(own, dim), (parts,), jnp.float32, smallest / len(pieces), top_value / len(pieces)))
        gain = gain * jnp.repeat(draws, dims[dim] // parts).reshape([-1 if axis == dim else 1 for axis in range(len(dims))])
    return gain


def routed_block(key, own, number, rows, number_of, top, reach, lean):
    order = jax.random.permutation(key, number_of)
    crowded, common = portions_of(number_of, rows * top, reach, lean, True), portions_of(number_of, rows * top, reach, lean, False)
    places = jnp.arange(number_of)

    def named(lengths, offset_by):
        used = int((lengths > 0).sum())
        fixed = max(1, used // 4)
        shifted = fixed + (places - fixed + offset_by * (used - fixed)) % max(1, number_of - fixed)
        return jnp.zeros((number_of,), jnp.int32).at[order[jnp.where(places < fixed, places, shifted)]].set(jnp.asarray(lengths, jnp.int32))

    lengths = jnp.where(number % 4 == 0, named(crowded, number // 4), named(common, number - number // 4 - 1))
    mixed = jax.random.permutation(jax.random.fold_in(own, 3), number_of)
    source_of, taker = mixed[0:number_of // 2 * 2:2], mixed[1:number_of // 2 * 2:2]
    margin = jnp.minimum(lengths[source_of] - 1, reach - lengths[taker]) // 2
    margin = jnp.where((source_of == order[0]) | (taker == order[0]) | (lengths[taker] == 0), 0, jnp.maximum(margin, 0))
    shifted = jax.random.randint(jax.random.fold_in(own, 4), (number_of // 2,), 0, 1 << 20) % (margin + 1)
    lengths = lengths.at[source_of].add(-shifted).at[taker].add(shifted)
    labels = jnp.searchsorted(jnp.cumsum(lengths), jnp.arange(rows * top), side="right").astype(jnp.int32)
    listing = labels.reshape(top, rows).T
    listing = listing[jax.random.permutation(jax.random.fold_in(own, 1), rows)]
    offset_by = jax.random.randint(jax.random.fold_in(own, 2), (rows, 1), 0, top)
    return jnp.take_along_axis(listing, (jnp.arange(top)[None, :] + offset_by) % top, axis=1)


def portions_of(amount, total, reach, skew, full):
    loads = [(1 << 20) // math.isqrt(standing ** skew) + 1 for standing in range(1, amount + 1)]
    largest = reach if full else min(reach, max(-(-total // amount), total * loads[0] // sum(loads)))
    least = 1 if total - largest >= amount - 1 else 0
    counts, rest = [largest] + [least] * (amount - 1), total - largest - least * (amount - 1)
    while rest > 0:
        free = [i for i in range(1, amount) if counts[i] < largest] or [i for i in range(1, amount) if counts[i] < reach]
        mass, left = sum([loads[i] for i in free]), rest
        for i in free:
            addition = min(reach - counts[i], max(1, left * loads[i] // mass), rest)
            counts[i] = counts[i] + addition
            rest = rest - addition
    return np.array(counts)


def normal_values(own_key, shape, width, bound, split=(), kind=jnp.bfloat16):
    values = width * jax.random.normal(own_key, shape, jnp.float32)
    if split:
        values = values * level_of(own_key, shape, split, -0.22, 0.18)
    return jnp.clip(values, -bound, bound).astype(kind)


def bell_draw_with(own_key, dims, deviation, reach, shards, heavy, kind=jnp.bfloat16):
    result = deviation * jax.random.normal(own_key, dims, jnp.float32)
    if shards:
        result = result * level_of(own_key, dims, shards, -0.22, 0.18)
    return jnp.clip(raised(result, jax.random.fold_in(own_key, 3), *heavy), -reach, reach).astype(kind)


def setup_inputs(seed: int = 0) -> dict:
    key_list = jax.random.split(jax.random.key(seed), 7)
    tokens = normal_values(key_list[0], (TOKENS, D), 1.0, 6.0, ((0, 64),))
    expert_ids_keys = jax.random.split(jax.random.fold_in(key_list[1], 1), TOKENS // TOK_EP)
    expert_ids_turns = jax.random.permutation(jax.random.fold_in(key_list[1], 3), TOKENS // TOK_EP)
    expert_ids = jax.vmap(lambda own, number: routed_block(jax.random.fold_in(key_list[1], 2), own, number, TOK_EP, EXPERTS, TOP, CAP, 2))(expert_ids_keys, expert_ids_turns).reshape((TOKENS, TOP))
    gate_scores = jnp.clip(0.1 + 0.9 * jax.random.uniform(key_list[2], (TOKENS, TOP), jnp.float32) ** level_of(key_list[2], (TOKENS, TOP), ((0, 64),), -0.2, 0.2), 0.1, 1.0)
    gate_weight = normal_values(key_list[3], (EXPERTS, D, FF), D ** -0.5, 0.09375, ((0, 64), (2, 8)))
    up_weight = normal_values(key_list[4], (EXPERTS, D, FF), D ** -0.5, 0.09375, ((0, 64), (2, 8)))
    down_weight = bell_draw_with(key_list[5], (EXPERTS, FF, D), FF ** -0.5, 0.25, ((0, 64), (1, 8)), (1, 2, 8, 2.0))
    return {"tokens": tokens, "expert_ids": expert_ids, "gate_scores": gate_scores, "gate_weight": gate_weight, "up_weight": up_weight, "down_weight": down_weight}


def places(block_ids, experts):
    one_hot = (block_ids[:, None] == jnp.arange(experts, dtype=jnp.int32)[None, :]).astype(jnp.int32)
    earlier = jnp.cumsum(one_hot, axis=0) - one_hot
    return jnp.sum(earlier * one_hot, axis=1).astype(jnp.int32)


def reference(tokens, expert_ids, gate_scores, gate_weight, up_weight, down_weight):
    block_ids = expert_ids.reshape(N_EP, TOK_EP * TOP)
    position = jax.vmap(lambda block_row: places(block_row, EXPERTS))(block_ids)
    source_block = jnp.arange(N_EP, dtype=jnp.int32)[:, None]
    slot_index = (source_block * CAP + position).reshape(-1).astype(jnp.int32)
    expert_of = expert_ids.reshape(-1).astype(jnp.int32)
    token_index = (jnp.arange(TOKENS * TOP, dtype=jnp.int32) // TOP).astype(jnp.int32)
    buffer = jnp.zeros((EXPERTS, N_EP * CAP, D), jnp.bfloat16).at[expert_of, slot_index].set(tokens[token_index])
    hidden_share = FF // N_HS

    def apply_expert(expert_item):
        slot_rows, gate_matrix, up_matrix, down_matrix = expert_item
        gate_act = jnp.dot(slot_rows, gate_matrix, preferred_element_type=jnp.float32)
        up_act = jnp.dot(slot_rows, up_matrix, preferred_element_type=jnp.float32)
        hidden = (jax.nn.silu(gate_act) * up_act).astype(jnp.bfloat16)
        hidden_blocks = hidden.reshape(-1, N_HS, hidden_share).transpose(1, 0, 2).astype(jnp.float32)
        down_blocks = down_matrix.reshape(N_HS, hidden_share, D).astype(jnp.float32)
        partials = jnp.einsum("hrf,hfd->hrd", hidden_blocks, down_blocks)
        rounded = lax.optimization_barrier(partials.astype(jnp.bfloat16))
        return jnp.sum(rounded.astype(jnp.float32), axis=0).astype(jnp.bfloat16)

    expert_outs = lax.map(apply_expert, (buffer, gate_weight, up_weight, down_weight))
    picked = expert_outs[expert_of, slot_index].reshape(TOKENS, TOP, D).astype(jnp.float32)
    mixed = jnp.sum(picked * gate_scores.astype(jnp.float32)[:, :, None], axis=1)
    return mixed.astype(jnp.bfloat16)
```

```python
import functools

import jax
import jax.numpy as jnp
from jax import lax
from jax.experimental import pallas as pl
from jax.experimental.pallas import tpu as pltpu
from jax.sharding import PartitionSpec as P

MESH = pl.DeviceIdType.MESH
F32, BF16 = jnp.float32, jnp.bfloat16


def dot(a, b):
    return jnp.dot(a, b, preferred_element_type=F32)


def iota(shape, dim):
    return lax.broadcasted_iota(jnp.int32, shape, dim)


def kernel(ne, nh, cap, parts,
           tok_hbm, ids_ref, score_ref, wg_hbm, wu_hbm, wd_hbm, out_ref,
           tok_v, xs, xb, wgu, wdt, acc, hb, ys, yb, yacc,
           local_sem, self_sem, xs_send, xs_recv, wd_send, wd_recv,
           ring_send, ring_recv, hid_send, hid_recv, y_send, y_recv):
    me = lax.axis_index("ep")
    z = lax.axis_index("hs")
    tokens, top = ids_ref.shape
    width = tok_v.shape[-1]
    units = wd_hbm.shape[1]
    half = nh // 2
    rows = ne * cap
    up_z, down_z = lax.rem(z + 1, nh), lax.rem(z + nh - 1, nh)
    far = lax.rem(z + half, nh)

    def plane(step):
        return lax.rem(z + step + nh, nh)

    barrier = pltpu.get_barrier_semaphore()

    def greet_ep(j, c):
        pl.semaphore_signal(barrier, inc=1, device_id={"ep": lax.rem(me + j, ne)}, device_id_type=MESH)
        return c

    def greet_hs(j, c):
        pl.semaphore_signal(barrier, inc=1, device_id={"hs": lax.rem(z + j, nh)}, device_id_type=MESH)
        return c

    lax.fori_loop(1, ne, greet_ep, 0)
    lax.fori_loop(1, nh, greet_hs, 0)

    def columns(s):
        return pl.ds(pl.multiple_of(s * width, width), width)

    loads = [
        pltpu.make_async_copy(tok_hbm.at[:, columns(z)], tok_v.at[0], local_sem.at[0]),
        pltpu.make_async_copy(tok_hbm.at[:, columns(far)], tok_v.at[1], local_sem.at[1]),
        pltpu.make_async_copy(wg_hbm.at[0], wgu.at[:, pl.ds(0, units)], local_sem.at[2]),
        pltpu.make_async_copy(wu_hbm.at[0], wgu.at[:, pl.ds(units, units)], local_sem.at[3]),
        pltpu.make_async_copy(wd_hbm.at[0, :, columns(z)], wdt.at[z], local_sem.at[4]),
    ]
    for load in loads:
        load.start()

    ids = ids_ref[...]
    gates = score_ref[...]
    named = jnp.zeros((tokens, ne), F32)
    score = jnp.zeros((tokens, ne), F32)
    lane = iota((tokens, ne), 1)
    for k in range(top):
        hit = ids[:, k:k + 1] == lane
        named = named + jnp.where(hit, 1.0, 0.0)
        score = score + jnp.where(hit, gates[:, k:k + 1], 0.0)
    before = jnp.where(iota((tokens, tokens), 1) < iota((tokens, tokens), 0), 1.0, 0.0).astype(BF16)
    place = dot(before, named.astype(BF16))
    mark = (named * (place + 1.0)).astype(BF16)
    spread = jnp.where(iota((rows, ne), 0) // cap == iota((rows, ne), 1), 1.0, 0.0).astype(BF16)
    nt = (((1,), (1,)), ((), ()))
    mark_rows = lax.dot_general(spread, mark, nt, preferred_element_type=F32)
    slot_row = (iota((rows, tokens), 0) % cap + 1).astype(F32)
    pick = jnp.where(mark_rows == slot_row, 1.0, 0.0).astype(BF16)

    loads[0].wait()
    xs[0] = dot(pick, tok_v[0]).reshape(ne, cap, width).astype(BF16)
    loads[1].wait()
    xs[1] = dot(pick, tok_v[1]).reshape(ne, cap, width).astype(BF16)

    mark_cols = lax.dot_general(mark, spread, nt, preferred_element_type=F32)
    slot_col = (iota((tokens, rows), 1) % cap + 1).astype(F32)
    score_high = score.astype(BF16)
    score_low = (score - score_high.astype(F32)).astype(BF16)
    here = mark_cols == slot_col
    gate_high = jnp.where(
        here, lax.dot_general(score_high, spread, nt, preferred_element_type=F32), 0.0).astype(BF16)
    gate_low = jnp.where(
        here, lax.dot_general(score_low, spread, nt, preferred_element_type=F32), 0.0).astype(BF16)

    pl.semaphore_wait(barrier, ne - 1 + nh - 1)

    def send_rows(q, s):
        def body(j, c):
            dest = lax.rem(me + j * 27, ne)
            pltpu.make_async_remote_copy(
                src_ref=xs.at[q, dest], dst_ref=xb.at[s, me],
                send_sem=xs_send.at[q], recv_sem=xs_recv.at[q],
                device_id={"ep": dest}, device_id_type=MESH).start()
            return c
        lax.fori_loop(1, ne, body, 0)

    send_rows(0, z)
    self_copies = [
        pltpu.make_async_copy(xs.at[0, me], xb.at[z, me], self_sem.at[0]),
        pltpu.make_async_copy(xs.at[1, me], xb.at[far, me], self_sem.at[1]),
    ]
    for copy in self_copies:
        copy.start()

    def send_down(j, c):
        dest = lax.rem(z + j, nh)
        pltpu.make_async_remote_copy(
            src_ref=wd_hbm.at[0, :, columns(dest)], dst_ref=wdt.at[z],
            send_sem=wd_send, recv_sem=wd_recv,
            device_id={"hs": dest}, device_id_type=MESH).start()
        return c

    lax.fori_loop(1, nh, send_down, 0)
    send_rows(1, far)

    def all_but_own(ref, sem):
        view = ref.at[pl.ds(0, ref.shape[0] - 1)]
        return pltpu.make_async_copy(view, view, sem)

    group = ne // parts
    chunk = group * cap

    def ring(direction, step, part):
        s = plane(-step) if direction == 0 else plane(step)
        view = xb.at[s, pl.ds(part * group, group)]
        return pltpu.make_async_remote_copy(
            src_ref=view, dst_ref=view,
            send_sem=ring_send.at[direction, step, part], recv_sem=ring_recv.at[direction, step, part],
            device_id={"hs": up_z if direction == 0 else down_z}, device_id_type=MESH)

    def arrived(direction, step, part):
        s = plane(-1 - step) if direction == 0 else plane(1 + step)
        view = xb.at[s, pl.ds(part * group, group)]
        return s, pltpu.make_async_copy(view, view, ring_recv.at[direction, step, part])

    def weights(s):
        return wgu[pl.ds(pl.multiple_of(s * width, width), width), :]

    def rows_of(s, part):
        return xb[s, pl.ds(part * group, group)].reshape(chunk, width)

    self_copies[0].wait()
    all_but_own(xb.at[z], xs_recv.at[0]).wait()

    steps = half - 1

    def start_ring(part, c):
        ring(0, 0, part).start()
        ring(1, 0, part).start()
        return c

    lax.fori_loop(0, parts, start_ring, 0)
    loads[2].wait()
    loads[3].wait()

    def first(part, c):
        acc[pl.ds(part * chunk, chunk), :] = dot(rows_of(z, part), weights(z))
        return c

    lax.fori_loop(0, parts, first, 0)

    for step in range(steps):
        def body(part, c, step=step):
            s_up, got_up = arrived(0, step, part)
            got_up.wait()
            if step + 1 < steps:
                ring(0, step + 1, part).start()
            s_down, got_down = arrived(1, step, part)
            got_down.wait()
            if step + 1 < steps:
                ring(1, step + 1, part).start()
            acc[pl.ds(part * chunk, chunk), :] += (
                dot(rows_of(s_up, part), weights(s_up)) + dot(rows_of(s_down, part), weights(s_down)))
            return c
        lax.fori_loop(0, parts, body, 0)
        if step == 0:
            self_copies[1].wait()
            all_but_own(xb.at[far], xs_recv.at[1]).wait()

            def second(part, c):
                acc[pl.ds(part * chunk, chunk), :] += dot(rows_of(far, part), weights(far))
                return c

            lax.fori_loop(0, parts, second, 0)

    hrows = rows // 2

    def hid(direction, step, part):
        s = plane(-step) if direction == 0 else plane(step)
        view = hb.at[s, pl.ds(part * hrows, hrows)]
        return pltpu.make_async_remote_copy(
            src_ref=view, dst_ref=view,
            send_sem=hid_send.at[direction, step, part], recv_sem=hid_recv.at[direction, step, part],
            device_id={"hs": up_z if direction == 0 else down_z}, device_id_type=MESH)

    def hid_arrived(direction, step, part):
        s = plane(-1 - step) if direction == 0 else plane(1 + step)
        view = hb.at[s, pl.ds(part * hrows, hrows)]
        return s, pltpu.make_async_copy(view, view, hid_recv.at[direction, step, part])

    for part in range(2):
        gate = acc[part * hrows:(part + 1) * hrows, 0:units]
        upper = acc[part * hrows:(part + 1) * hrows, units:2 * units]
        hb[z, part * hrows:(part + 1) * hrows, :] = (
            gate / (1.0 + jnp.exp(-gate)) * upper).astype(BF16)
        hid(0, 0, part).start()
        hid(1, 0, part).start()

    loads[4].wait()
    all_but_own(wdt, wd_recv).wait()

    def out_part(s, part):
        return dot(hb[s, part * hrows:(part + 1) * hrows, :], wdt[s])

    for part in range(2):
        yacc[part * hrows:(part + 1) * hrows, :] = out_part(z, part)
    for step in range(steps):
        for part in range(2):
            s_up, got_up = hid_arrived(0, step, part)
            s_down, got_down = hid_arrived(1, step, part)
            got_up.wait()
            if step + 1 < steps or part == 0:
                hid(0, step + 1, part).start()
            got_down.wait()
            if step + 1 < steps or part == 1:
                hid(1, step + 1, part).start()
            yacc[part * hrows:(part + 1) * hrows, :] += out_part(s_up, part) + out_part(s_down, part)

    half_blocks = ne // 2
    for part in range(2):
        _, got = hid_arrived(part, steps, part)
        got.wait()
        total = yacc[part * hrows:(part + 1) * hrows, :] + out_part(far, part)
        ys[part * half_blocks:(part + 1) * half_blocks] = (
            total.reshape(half_blocks, cap, width).astype(BF16))

        def send_back(j, c, part=part):
            dest = part * half_blocks + lax.rem(me + j * 11, half_blocks)

            @pl.when(dest != me)
            def _():
                pltpu.make_async_remote_copy(
                    src_ref=ys.at[dest], dst_ref=yb.at[me],
                    send_sem=y_send, recv_sem=y_recv,
                    device_id={"ep": dest}, device_id_type=MESH).start()
            return c

        lax.fori_loop(0, half_blocks, send_back, 0)

    own = pltpu.make_async_copy(ys.at[me], yb.at[me], self_sem.at[2])
    own.start()
    own.wait()
    all_but_own(yb, y_recv).wait()
    back = yb[...].reshape(rows, width)
    out_ref[...] = (dot(gate_high, back) + dot(gate_low, back)).astype(BF16)

    for q in range(2):
        all_but_own(xs.at[q], xs_send.at[q]).wait()
    all_but_own(wdt, wd_send).wait()
    all_but_own(ys, y_send).wait()

    def drain(part, c):
        for direction in range(2):
            for step in range(steps):
                ring(direction, step, part).wait_send()
        return c

    lax.fori_loop(0, parts, drain, 0)
    for direction in range(2):
        for part in range(2):
            for step in range(steps):
                hid(direction, step, part).wait_send()
        hid(direction, steps, direction).wait_send()


def local(tokens, expert_ids, gate_scores, gate_weight, up_weight, down_weight):
    ne, nh = lax.axis_size("ep"), lax.axis_size("hs")
    count, model = tokens.shape
    width = model // nh
    units = gate_weight.shape[2]
    cap = max(2, 2 * expert_ids.shape[1] * count // ne)
    rows = ne * cap
    parts = 4
    steps = nh // 2 - 1
    dma = pltpu.SemaphoreType.DMA
    anywhere = pl.BlockSpec(memory_space=pl.ANY)
    vmem = pl.BlockSpec(memory_space=pltpu.VMEM)
    return pl.pallas_call(
        functools.partial(kernel, ne, nh, cap, parts),
        out_shape=jax.ShapeDtypeStruct((count, width), BF16),
        in_specs=[anywhere, vmem, vmem, anywhere, anywhere, anywhere],
        out_specs=vmem,
        scratch_shapes=[
            pltpu.VMEM((2, count, width), BF16),
            pltpu.VMEM((2, ne, cap, width), BF16),
            pltpu.VMEM((nh, ne, cap, width), BF16),
            pltpu.VMEM((model, 2 * units), BF16),
            pltpu.VMEM((nh, units, width), BF16),
            pltpu.VMEM((rows, 2 * units), F32),
            pltpu.VMEM((nh, rows, units), BF16),
            pltpu.VMEM((ne, cap, width), BF16),
            pltpu.VMEM((ne, cap, width), BF16),
            pltpu.VMEM((rows, width), F32),
            dma((5,)), dma((3,)), dma((2,)), dma((2,)), dma, dma,
            dma((2, steps, parts)), dma((2, steps, parts)),
            dma((2, steps + 1, 2)), dma((2, steps + 1, 2)), dma, dma,
        ],
        compiler_params=pltpu.CompilerParams(
            collective_id=0, has_side_effects=True, vmem_limit_bytes=48 << 20),
    )(tokens, expert_ids, gate_scores, gate_weight, up_weight, down_weight)


def solution(mesh):
    placed = (
        P("ep", None),
        P("ep", None),
        P("ep", None),
        P("ep", None, "hs"),
        P("ep", None, "hs"),
        P("ep", "hs", None),
    )
    return jax.shard_map(
        local, mesh=mesh, in_specs=placed, out_specs=P("ep", "hs"), check_vma=False
    )
```

```python
import functools

import jax
import jax.numpy as jnp
from jax import lax
from jax.experimental import pallas as pl
from jax.experimental.pallas import tpu as pltpu
from jax.sharding import PartitionSpec as P

MESH = pl.DeviceIdType.MESH
F32, BF16 = jnp.float32, jnp.bfloat16
CHIPS_Y, CORES = 8, 2


def dot(a, b):
    return jnp.dot(a, b, preferred_element_type=F32)


def dot_nt(a, b):
    return lax.dot_general(a, b, (((1,), (1,)), ((), ())), preferred_element_type=F32)


def iota(shape, dim):
    return lax.broadcasted_iota(jnp.int32, shape, dim)


def ones_where(condition):
    return jnp.where(condition, 1.0, 0.0).astype(BF16)


def kernel(ne, nh, ny, cap, slices,
           tok_hbm, ids_ref, score_ref, wg_hbm, wu_hbm, wd_hbm, out_ref,
           tok_v, mk, mb, tb, pick, xs, xb, wgu, wdt, acc, hb, ys, yb, yacc,
           load_sem, own_sem, self_sem, mk_send, mk_recv, tok_send, tok_recv, x_send, x_recv,
           wd_send, wd_recv, ring_send, ring_recv, hid_send, hid_recv, y_send, y_recv):
    me = lax.axis_index("ep")
    z = lax.axis_index("hs")
    nc = CORES
    nx = ne // (ny * nc)
    c = lax.rem(me, nc)
    y = lax.rem(me // nc, ny)
    x = me // (nc * ny)
    top, tokens = ids_ref.shape
    width = yacc.shape[-1]
    part_width = width // nc
    units = wd_hbm.shape[1]
    half = nh // 2
    rows = ne * cap
    nq = ny * nc
    nd = nx * nc
    q = lax.rem(me, nq)
    d = x * nc + c
    count = len(slices)
    up_z, down_z = lax.rem(z + 1, nh), lax.rem(z + nh - 1, nh)
    far = lax.rem(z + half, nh)

    def plane(step):
        return lax.rem(z + step + nh, nh)

    barrier = pltpu.get_barrier_semaphore()

    def greet_ep(j, carry):
        pl.semaphore_signal(barrier, inc=1, device_id={"ep": lax.rem(me + j, ne)}, device_id_type=MESH)
        return carry

    def greet_hs(j, carry):
        pl.semaphore_signal(barrier, inc=1, device_id={"hs": lax.rem(z + j, nh)}, device_id_type=MESH)
        return carry

    lax.fori_loop(1, ne, greet_ep, 0)
    lax.fori_loop(1, nh, greet_hs, 0)

    def columns(s):
        return pl.ds(pl.multiple_of(s * width, width), width)

    def part_columns(s, part):
        return pl.ds(pl.multiple_of(s * width + part * part_width, part_width), part_width)

    loads = [
        pltpu.make_async_copy(tok_hbm, tok_v, load_sem.at[0]),
        pltpu.make_async_copy(wg_hbm.at[0], wgu.at[:, pl.ds(0, units)], load_sem.at[1]),
        pltpu.make_async_copy(wu_hbm.at[0], wgu.at[:, pl.ds(units, units)], load_sem.at[2]),
        pltpu.make_async_copy(wd_hbm.at[0, :, columns(z)], wdt.at[z], load_sem.at[3]),
    ]
    own_tokens = [
        pltpu.make_async_copy(tok_hbm.at[:, part_columns(plane(rel), c)], tb.at[r, q], own_sem.at[r])
        for r, rel in enumerate(slices)
    ]
    for load in loads[:1] + own_tokens + loads[1:]:
        load.start()

    ids = ids_ref[...]
    gates = score_ref[...]
    order = iota((ne, tokens), 0)
    expert = (lax.rem(order, nd) // nc * ny + order // nd) * nc + lax.rem(order, nc)
    named = jnp.zeros((ne, tokens), F32)
    score = jnp.zeros((ne, tokens), F32)
    for k in range(top):
        hit = ids[k:k + 1, :] == expert
        named = named + jnp.where(hit, 1.0, 0.0)
        score = score + jnp.where(hit, gates[k:k + 1, :], 0.0)
    before = ones_where(iota((tokens, tokens), 0) < iota((tokens, tokens), 1))
    mark = (named * (dot(named.astype(BF16), before) + 1.0)).astype(BF16)
    per_group = 128 // tokens
    shift = ones_where(
        iota((tokens, 128), 1) == iota((tokens, 128), 0) + lax.rem(q, per_group) * tokens)
    mk[...] = dot(mark, shift).reshape(ny, nd, 128)

    loads[0].wait()
    pl.semaphore_wait(barrier, ne - 1 + nh - 1)

    def along_y(j):
        other = lax.rem(q + j, nq)
        return other, {"ep": x * nq + other}

    def send_tokens(r, rel):
        def body(j, carry):
            other, device = along_y(j)
            pltpu.make_async_remote_copy(
                src_ref=tok_v.at[:, part_columns(plane(rel), lax.rem(other, nc))], dst_ref=tb.at[r, q],
                send_sem=tok_send.at[r], recv_sem=tok_recv.at[r],
                device_id=device, device_id_type=MESH).start()
            return carry
        lax.fori_loop(1, nq, body, 0)

    def send_marks(j, carry):
        other, device = along_y(j)
        pltpu.make_async_remote_copy(
            src_ref=mk.at[other // nc], dst_ref=mb.at[q], send_sem=mk_send, recv_sem=mk_recv,
            device_id=device, device_id_type=MESH).start()
        return carry

    lax.fori_loop(1, nq, send_marks, 0)
    own_marks = pltpu.make_async_copy(mk.at[y], mb.at[q], self_sem.at[0])
    own_marks.start()
    send_tokens(0, slices[0])

    def send_down(j, carry):
        dest = lax.rem(z + j, nh)
        pltpu.make_async_remote_copy(
            src_ref=wd_hbm.at[0, :, columns(dest)], dst_ref=wdt.at[z],
            send_sem=wd_send, recv_sem=wd_recv,
            device_id={"hs": dest}, device_id_type=MESH).start()
        return carry

    lax.fori_loop(1, nh, send_down, 0)
    for r in range(1, count):
        send_tokens(r, slices[r])

    spread = ones_where(iota((rows, ne), 0) // cap == iota((rows, ne), 1))
    here = dot(spread, mark) == (lax.rem(iota((rows, tokens), 0), cap) + 1).astype(F32)
    score_high = score.astype(BF16)
    score_low = (score - score_high.astype(F32)).astype(BF16)
    same = ones_where(iota((tokens, tokens), 0) == iota((tokens, tokens), 1))
    gate_high = dot_nt(same, jnp.where(here, dot(spread, score_high), 0.0).astype(BF16)).astype(BF16)
    gate_low = dot_nt(same, jnp.where(here, dot(spread, score_low), 0.0).astype(BF16)).astype(BF16)

    def bytes_of(view, sem):
        return pltpu.make_async_copy(view, view, sem)

    own_marks.wait()
    bytes_of(mb.at[pl.ds(0, nq - 1)], mk_recv).wait()
    marks = jnp.concatenate(
        [sum(mb[g * per_group + i] for i in range(per_group)) for g in range(nq // per_group)], axis=1)
    q_rows, q_lanes = nq * cap, nq * tokens
    slot = (lax.rem(iota((q_rows, q_lanes), 0), cap) + 1).astype(F32)
    slot = jnp.where(iota((q_rows, q_lanes), 0) // cap == iota((q_rows, q_lanes), 1) // tokens, slot, -1.0)
    for i in range(nd):
        pick[i] = ones_where(marks[i:i + 1, :] == slot)

    def select(r):
        own_tokens[r].wait()
        bytes_of(tb.at[r, pl.ds(0, nq - 1)], tok_recv.at[r]).wait()
        block = tb[r].reshape(q_lanes, part_width)
        s = plane(slices[r])

        def body(j, carry):
            i = lax.rem(d + j, nd)
            xs[r, i] = dot(pick[i], block).astype(BF16)
            pltpu.make_async_remote_copy(
                src_ref=xs.at[r, i],
                dst_ref=xb.at[s, x, :, pl.ds(pl.multiple_of(c * part_width, part_width), part_width)],
                send_sem=x_send.at[r], recv_sem=x_recv.at[r],
                device_id={"ep": (i // nc * ny + y) * nc + lax.rem(i, nc)}, device_id_type=MESH).start()
            return carry

        lax.fori_loop(1, nd, body, 0)
        xb[s, x, :, pl.ds(pl.multiple_of(c * part_width, part_width), part_width)] = (
            dot(pick[d], block).astype(BF16))

    def weights(s):
        return wgu[pl.ds(pl.multiple_of(s * width, width), width), :]

    def multiply(s, first=False):
        product = dot(xb[s].reshape(rows, width), weights(s))
        if first:
            acc[...] = product
        else:
            acc[...] += product

    def ring(direction, part):
        view = xb.at[z, part]
        return pltpu.make_async_remote_copy(
            src_ref=view, dst_ref=view,
            send_sem=ring_send.at[direction, part], recv_sem=ring_recv.at[direction, part],
            device_id={"hs": up_z if direction == 0 else down_z}, device_id_type=MESH)

    def collect(r):
        bytes_of(xs.at[r, pl.ds(0, nd - 1)], x_recv.at[r]).wait()
        if r == 0:
            for part in range(nx):
                ring(0, part).start()
                ring(1, part).start()
            loads[1].wait()
            loads[2].wait()
        multiply(plane(slices[r]), first=r == 0)

    select(0)
    for r in range(1, count):
        select(r)
        collect(r - 1)

    for direction, s in ((0, plane(-1)), (1, plane(1))):
        for part in range(nx):
            view = xb.at[s, part]
            bytes_of(view, ring_recv.at[direction, part]).wait()
        multiply(s)
    collect(count - 1)

    steps = half - 1
    hrows = rows // 2

    def hid(direction, step, part):
        s = plane(-step) if direction == 0 else plane(step)
        view = hb.at[s, pl.ds(part * hrows, hrows)]
        return pltpu.make_async_remote_copy(
            src_ref=view, dst_ref=view,
            send_sem=hid_send.at[direction, step, part], recv_sem=hid_recv.at[direction, step, part],
            device_id={"hs": up_z if direction == 0 else down_z}, device_id_type=MESH)

    def hid_arrived(direction, step, part):
        s = plane(-1 - step) if direction == 0 else plane(1 + step)
        view = hb.at[s, pl.ds(part * hrows, hrows)]
        return s, bytes_of(view, hid_recv.at[direction, step, part])

    for part in range(2):
        gate = acc[part * hrows:(part + 1) * hrows, 0:units]
        upper = acc[part * hrows:(part + 1) * hrows, units:2 * units]
        hb[z, part * hrows:(part + 1) * hrows, :] = (
            gate / (1.0 + jnp.exp(-gate)) * upper).astype(BF16)
        hid(0, 0, part).start()
        hid(1, 0, part).start()

    loads[3].wait()
    bytes_of(wdt.at[pl.ds(0, nh - 1)], wd_recv).wait()

    def out_part(s, part):
        return dot(hb[s, part * hrows:(part + 1) * hrows, :], wdt[s])

    for part in range(2):
        yacc[part * hrows:(part + 1) * hrows, :] = out_part(z, part)
    for step in range(steps):
        for part in range(2):
            s_up, got_up = hid_arrived(0, step, part)
            s_down, got_down = hid_arrived(1, step, part)
            got_up.wait()
            if step + 1 < steps or part == 0:
                hid(0, step + 1, part).start()
            got_down.wait()
            if step + 1 < steps or part == 1:
                hid(1, step + 1, part).start()
            yacc[part * hrows:(part + 1) * hrows, :] += out_part(s_up, part) + out_part(s_down, part)

    half_blocks = ne // 2
    place = y * nd + d
    for part in range(2):
        _, got = hid_arrived(part, steps, part)
        got.wait()
        total = yacc[part * hrows:(part + 1) * hrows, :] + out_part(far, part)
        ys[part * half_blocks:(part + 1) * half_blocks] = (
            total.reshape(half_blocks, cap, width).astype(BF16))

        def send_back(j, carry, part=part):
            dest = part * half_blocks + lax.rem(me + j * 11, half_blocks)

            @pl.when(dest != me)
            def _():
                pltpu.make_async_remote_copy(
                    src_ref=ys.at[dest], dst_ref=yb.at[place],
                    send_sem=y_send, recv_sem=y_recv,
                    device_id={"ep": dest}, device_id_type=MESH).start()
            return carry

        lax.fori_loop(0, half_blocks, send_back, 0)

    own = pltpu.make_async_copy(ys.at[me], yb.at[place], self_sem.at[1])
    own.start()
    own.wait()
    bytes_of(yb.at[pl.ds(0, ne - 1)], y_recv).wait()
    back = yb[...].reshape(rows, width)
    out_ref[...] = (dot(gate_high, back) + dot(gate_low, back)).astype(BF16)

    bytes_of(mb.at[pl.ds(0, nq - 1)], mk_send).wait()
    for r in range(count):
        bytes_of(tb.at[r, pl.ds(0, nq - 1)], tok_send.at[r]).wait()
        bytes_of(xs.at[r, pl.ds(0, nd - 1)], x_send.at[r]).wait()
    bytes_of(wdt.at[pl.ds(0, nh - 1)], wd_send).wait()
    bytes_of(ys.at[pl.ds(0, ne - 1)], y_send).wait()
    for direction in range(2):
        for part in range(nx):
            ring(direction, part).wait_send()
        for part in range(2):
            for step in range(steps):
                hid(direction, step, part).wait_send()
        hid(direction, steps, direction).wait_send()


def local(tokens, expert_ids, gate_scores, gate_weight, up_weight, down_weight):
    ne, nh, ny = lax.axis_size("ep"), lax.axis_size("hs"), CHIPS_Y
    count, model = tokens.shape
    width = model // nh
    part_width = width // CORES
    units = gate_weight.shape[2]
    cap = max(2, 2 * expert_ids.shape[1] * count // ne)
    rows = ne * cap
    nq, nd, nx = ny * CORES, ne // ny, ne // (ny * CORES)
    slices = (0,) + tuple(range(2, nh - 1))
    rounds = len(slices)
    steps = nh // 2 - 1
    dma = pltpu.SemaphoreType.DMA
    hbm = pl.BlockSpec(memory_space=pltpu.MemorySpace.HBM)
    vmem = pl.BlockSpec(memory_space=pltpu.MemorySpace.VMEM)
    return pl.pallas_call(
        functools.partial(kernel, ne, nh, ny, cap, slices),
        out_shape=jax.ShapeDtypeStruct((count, width), BF16),
        in_specs=[hbm, vmem, vmem, hbm, hbm, hbm],
        out_specs=vmem,
        scratch_shapes=[
            pltpu.VMEM((count, model), BF16),
            pltpu.VMEM((ny, nd, 128), F32),
            pltpu.VMEM((nq, nd, 128), F32),
            pltpu.VMEM((rounds, nq, count, part_width), BF16),
            pltpu.VMEM((nd, nq * cap, nq * count), BF16),
            pltpu.VMEM((rounds, nd, nq * cap, part_width), BF16),
            pltpu.VMEM((nh, nx, nq * cap, width), BF16),
            pltpu.VMEM((model, 2 * units), BF16),
            pltpu.VMEM((nh, units, width), BF16),
            pltpu.VMEM((rows, 2 * units), F32),
            pltpu.VMEM((nh, rows, units), BF16),
            pltpu.VMEM((ne, cap, width), BF16),
            pltpu.VMEM((ne, cap, width), BF16),
            pltpu.VMEM((rows, width), F32),
            dma((4,)), dma((rounds,)), dma((2,)), dma, dma, dma((rounds,)), dma((rounds,)),
            dma((rounds,)), dma((rounds,)), dma, dma,
            dma((2, nx)), dma((2, nx)),
            dma((2, steps + 1, 2)), dma((2, steps + 1, 2)), dma, dma,
        ],
        compiler_params=pltpu.CompilerParams(
            collective_id=0, has_side_effects=True, vmem_limit_bytes=63 << 20),
    )(tokens, expert_ids.T, gate_scores.T, gate_weight, up_weight, down_weight)


def solution(mesh):
    placed = (
        P("ep", None),
        P("ep", None),
        P("ep", None),
        P("ep", None, "hs"),
        P("ep", None, "hs"),
        P("ep", "hs", None),
    )
    return jax.shard_map(
        local, mesh=mesh, in_specs=placed, out_specs=P("ep", "hs"), check_vma=False
    )
```

```python
import functools

import jax
import jax.numpy as jnp
from jax import lax
from jax.experimental import pallas as pl
from jax.experimental.pallas import tpu as pltpu
from jax.sharding import PartitionSpec as P

MESH = pl.DeviceIdType.MESH
F32, BF16 = jnp.float32, jnp.bfloat16
CHIPS_Y, CORES = 8, 2


def dot(a, b):
    return jnp.dot(a, b, preferred_element_type=F32)


def dot_nt(a, b):
    return lax.dot_general(a, b, (((1,), (1,)), ((), ())), preferred_element_type=F32)


def iota(shape, dim):
    return lax.broadcasted_iota(jnp.int32, shape, dim)


def ones_where(condition):
    return jnp.where(condition, 1.0, 0.0).astype(BF16)


def kernel(ne, nh, ny, cap, slices, late,
           tok_hbm, ids_ref, score_ref, wg_hbm, wu_hbm, wd_hbm, out_ref,
           tok_v, mk, mb, tb, pick, xs, xb, wgu, wdt, acc, hb, ys, yb, yacc,
           load_sem, own_sem, self_sem, mk_send, mk_recv, tok_send, tok_recv, x_send, x_recv,
           wd_send, wd_recv, ring_send, ring_recv, hid_send, hid_recv, y_send, y_recv):
    me = lax.axis_index("ep")
    z = lax.axis_index("hs")
    nc = CORES
    nx = ne // (ny * nc)
    c = lax.rem(me, nc)
    y = lax.rem(me // nc, ny)
    x = me // (nc * ny)
    top, tokens = ids_ref.shape
    width = yacc.shape[-1]
    part_width = width // nc
    units = wd_hbm.shape[1]
    half = nh // 2
    rows = ne * cap
    nq = ny * nc
    nd = nx * nc
    q = lax.rem(me, nq)
    d = x * nc + c
    count = len(slices)
    offsets = (0,) + tuple(o for i in range(1, nx // 2) for o in (i, nx - i)) + (nx // 2,)
    chunks = [lax.rem(x + offset, nx) for offset in offsets]
    up_z, down_z = lax.rem(z + 1, nh), lax.rem(z + nh - 1, nh)
    far = lax.rem(z + half, nh)

    def plane(step):
        return lax.rem(z + step + nh, nh)

    barrier = pltpu.get_barrier_semaphore()

    def greet_ep(j, carry):
        pl.semaphore_signal(barrier, inc=1, device_id={"ep": lax.rem(me + j, ne)}, device_id_type=MESH)
        return carry

    def greet_hs(j, carry):
        pl.semaphore_signal(barrier, inc=1, device_id={"hs": lax.rem(z + j, nh)}, device_id_type=MESH)
        return carry

    lax.fori_loop(1, ne, greet_ep, 0)
    lax.fori_loop(1, nh, greet_hs, 0)

    def routed(r, core):
        base, by_core = slices[r]
        return plane(base + by_core * core)

    def columns(s):
        return pl.ds(pl.multiple_of(s * width, width), width)

    def part_columns(s, part):
        return pl.ds(pl.multiple_of(s * width + part * part_width, part_width), part_width)

    loads = [
        pltpu.make_async_copy(tok_hbm, tok_v, load_sem.at[0]),
        pltpu.make_async_copy(wg_hbm.at[0], wgu.at[:, pl.ds(0, units)], load_sem.at[1]),
        pltpu.make_async_copy(wu_hbm.at[0], wgu.at[:, pl.ds(units, units)], load_sem.at[2]),
        pltpu.make_async_copy(wd_hbm.at[0, :, columns(z)], wdt.at[z], load_sem.at[3]),
    ]
    own_tokens = [
        pltpu.make_async_copy(tok_hbm.at[:, part_columns(routed(r, c), c)], tb.at[r, q], own_sem.at[r])
        for r in range(count)
    ]
    for load in loads[:1] + own_tokens + loads[1:]:
        load.start()

    ids = ids_ref[...]
    gates = score_ref[...]
    order = iota((ne, tokens), 0)
    expert = (lax.rem(order, nd) // nc * ny + order // nd) * nc + lax.rem(order, nc)
    named = jnp.zeros((ne, tokens), F32)
    score = jnp.zeros((ne, tokens), F32)
    for k in range(top):
        hit = ids[k:k + 1, :] == expert
        named = named + jnp.where(hit, 1.0, 0.0)
        score = score + jnp.where(hit, gates[k:k + 1, :], 0.0)
    before = ones_where(iota((tokens, tokens), 0) < iota((tokens, tokens), 1))
    mark = (named * (dot(named.astype(BF16), before) + 1.0)).astype(BF16)
    per_group = 128 // tokens
    shift = ones_where(
        iota((tokens, 128), 1) == iota((tokens, 128), 0) + lax.rem(q, per_group) * tokens)
    mk[...] = dot(mark, shift).reshape(ny, nd, 128)

    loads[0].wait()
    pl.semaphore_wait(barrier, ne - 1 + nh - 1)

    def along_y(j):
        other = lax.rem(q + j * 5, nq)
        return other, {"ep": x * nq + other}

    def send_tokens(r):
        def body(j, carry):
            other, device = along_y(j)
            pltpu.make_async_remote_copy(
                src_ref=tok_v.at[:, part_columns(routed(r, lax.rem(other, nc)), lax.rem(other, nc))],
                dst_ref=tb.at[r, q],
                send_sem=tok_send.at[r], recv_sem=tok_recv.at[r],
                device_id=device, device_id_type=MESH).start()
            return carry
        lax.fori_loop(1, nq, body, 0)

    def send_marks(j, carry):
        other, device = along_y(j)
        pltpu.make_async_remote_copy(
            src_ref=mk.at[other // nc], dst_ref=mb.at[q], send_sem=mk_send, recv_sem=mk_recv,
            device_id=device, device_id_type=MESH).start()
        return carry

    lax.fori_loop(1, nq, send_marks, 0)
    own_marks = pltpu.make_async_copy(mk.at[y], mb.at[q], self_sem.at[0])
    own_marks.start()
    send_tokens(0)

    def send_down(j, carry):
        dest = lax.rem(z + j, nh)
        pltpu.make_async_remote_copy(
            src_ref=wd_hbm.at[0, :, columns(dest)], dst_ref=wdt.at[z],
            send_sem=wd_send, recv_sem=wd_recv,
            device_id={"hs": dest}, device_id_type=MESH).start()
        return carry

    lax.fori_loop(half - 1, half + 2, send_down, 0)
    lax.fori_loop(1, half - 1, send_down, 0)
    lax.fori_loop(half + 2, nh, send_down, 0)
    for r in range(1, count):
        send_tokens(r)

    spread = ones_where(iota((rows, ne), 0) // cap == iota((rows, ne), 1))
    here = dot(spread, mark) == (lax.rem(iota((rows, tokens), 0), cap) + 1).astype(F32)
    score_high = score.astype(BF16)
    score_low = (score - score_high.astype(F32)).astype(BF16)
    same = ones_where(iota((tokens, tokens), 0) == iota((tokens, tokens), 1))
    gate_high = dot_nt(same, jnp.where(here, dot(spread, score_high), 0.0).astype(BF16)).astype(BF16)
    gate_low = dot_nt(same, jnp.where(here, dot(spread, score_low), 0.0).astype(BF16)).astype(BF16)

    def bytes_of(view, sem):
        return pltpu.make_async_copy(view, view, sem)

    own_marks.wait()
    bytes_of(mb.at[pl.ds(0, nq - 1)], mk_recv).wait()
    marks = jnp.concatenate(
        [sum(mb[g * per_group + i] for i in range(per_group)) for g in range(nq // per_group)], axis=1)
    q_rows, q_lanes = nq * cap, nq * tokens
    slot = (lax.rem(iota((q_rows, q_lanes), 0), cap) + 1).astype(F32)
    slot = jnp.where(iota((q_rows, q_lanes), 0) // cap == iota((q_rows, q_lanes), 1) // tokens, slot, -1.0)
    for i in range(nd):
        pick[i] = ones_where(marks[i:i + 1, :] == slot)

    def select(r):
        own_tokens[r].wait()
        bytes_of(tb.at[r, pl.ds(0, nq - 1)], tok_recv.at[r]).wait()
        block = tb[r].reshape(q_lanes, part_width)
        s = routed(r, c)

        def send_selected(i):
            xs[r, i] = dot(pick[i], block).astype(BF16)
            pltpu.make_async_remote_copy(
                src_ref=xs.at[r, i],
                dst_ref=xb.at[s, x, :, pl.ds(pl.multiple_of(c * part_width, part_width), part_width)],
                send_sem=x_send.at[r], recv_sem=x_recv.at[r, lax.rem(x - i // nc + nx, nx)],
                device_id={"ep": (i // nc * ny + y) * nc + lax.rem(i, nc)}, device_id_type=MESH).start()

        send_selected(x * nc + lax.rem(c + 1, nc))
        xb[s, x, :, pl.ds(pl.multiple_of(c * part_width, part_width), part_width)] = (
            dot(pick[d], block).astype(BF16))
        for offset in offsets[1:]:
            def body(j, carry, offset=offset):
                send_selected(lax.rem(x + offset, nx) * nc + j)
                return carry
            lax.fori_loop(0, nc, body, 0)

    def selected(r, offset):
        bytes_of(xs.at[r, pl.ds(0, nc if offset else nc - 1)], x_recv.at[r, offset]).wait()

    def weights(s):
        return wgu[pl.ds(pl.multiple_of(s * width, width), width), :]

    def multiply(s, first=False):
        product = dot(xb[s].reshape(rows, width), weights(s)).reshape(acc.shape)
        if first:
            acc[...] = product
        else:
            acc[...] += product

    def ring_view(s, step, direction, k):
        if step == 0:
            return xb.at[s, chunks[k]]
        return xb.at[s, chunks[k], :, pl.ds(direction * part_width, part_width)]

    def ring(direction, step, k):
        view = ring_view(plane(-step) if direction == 0 else plane(step), step, direction, k)
        return pltpu.make_async_remote_copy(
            src_ref=view, dst_ref=view,
            send_sem=ring_send.at[direction, step, k], recv_sem=ring_recv.at[direction, step, k],
            device_id={"hs": up_z if direction == 0 else down_z}, device_id_type=MESH)

    def ring_arrived(direction, step, k):
        s = plane(-1 - step) if direction == 0 else plane(1 + step)
        return bytes_of(ring_view(s, step, direction, k), ring_recv.at[direction, step, k])

    def collect(r):
        for offset in offsets:
            selected(r, offset)
        if r == 0:
            for k in range(nx):
                ring(0, 0, k).start()
                ring(1, 0, k).start()
            loads[1].wait()
            loads[2].wait()
        if slices[r][1] == 0:
            multiply(plane(slices[r][0]), first=r == 0)

    select(0)
    for r in range(1, count):
        select(r)
        if r < count - late + 1:
            collect(r - 1)

    for k in range(nx):
        for direction in range(2):
            ring_arrived(direction, 0, k).wait()
            ring(direction, 1, k).start()
    multiply(plane(-1))
    multiply(plane(1))

    steps = half - 1

    def antipode(k):
        return 0 if k < nx // 2 else 1

    def hid(direction, step, k):
        s = plane(-step) if direction == 0 else plane(step)
        view = hb.at[s, chunks[k]]
        return pltpu.make_async_remote_copy(
            src_ref=view, dst_ref=view,
            send_sem=hid_send.at[direction, step, k], recv_sem=hid_recv.at[direction, step, k],
            device_id={"hs": up_z if direction == 0 else down_z}, device_id_type=MESH)

    def hid_arrived(direction, step, k):
        s = plane(-1 - step) if direction == 0 else plane(1 + step)
        return s, bytes_of(hb.at[s, chunks[k]], hid_recv.at[direction, step, k])

    def out_part(s, k):
        return dot(hb[s, chunks[k]], wdt[s])

    def make_hidden(k):
        total = acc[chunks[k]]
        for direction, s in ((0, plane(-2)), (1, plane(2))):
            ring_arrived(direction, 1, k).wait()
            total = total + dot(xb[s, chunks[k]], weights(s))
        for r in range(count - late, count):
            selected(r, offsets[k])
            s = plane(slices[r][0])
            total = total + dot(xb[s, chunks[k]], weights(s))
        gate, upper = total[:, 0:units], total[:, units:2 * units]
        hb[z, chunks[k]] = (gate / (1.0 + jnp.exp(-gate)) * upper).astype(BF16)
        hid(0, 0, k).start()
        hid(1, 0, k).start()

    def pass_hidden(k, step):
        s_up, got_up = hid_arrived(0, step, k)
        s_down, got_down = hid_arrived(1, step, k)
        got_up.wait()
        if step + 1 < steps or antipode(k) == 0:
            hid(0, step + 1, k).start()
        got_down.wait()
        if step + 1 < steps or antipode(k) == 1:
            hid(1, step + 1, k).start()
        if step == 0:
            yacc[chunks[k]] = out_part(z, k) + out_part(s_up, k) + out_part(s_down, k)
        else:
            yacc[chunks[k]] += out_part(s_up, k) + out_part(s_down, k)

    place = y * nd + d

    def finish(k):
        _, got = hid_arrived(antipode(k), steps, k)
        got.wait()
        total = yacc[chunks[k]] + out_part(far, k)
        ys[pl.ds(chunks[k] * nq, nq)] = total.reshape(nq, cap, width).astype(BF16)

        def send_back(j, carry):
            dest = chunks[k] * nq + lax.rem(q + j * 5, nq)
            pltpu.make_async_remote_copy(
                src_ref=ys.at[dest], dst_ref=yb.at[place],
                send_sem=y_send, recv_sem=y_recv,
                device_id={"ep": dest}, device_id_type=MESH).start()
            return carry

        lax.fori_loop(1 if k == 0 else 0, nq, send_back, 0)

    make_hidden(0)
    loads[3].wait()
    for k in range(1, nx):
        make_hidden(k)
        if k == 1:
            bytes_of(wdt.at[pl.ds(0, nh - 1)], wd_recv).wait()
        if k <= steps:
            pass_hidden(0, k - 1)
    for step in range(nx - 1, steps):
        pass_hidden(0, step)
    for k in range(1, nx):
        pass_hidden(k, 0)
    finish(0)
    for step in range(1, steps):
        for k in range(1, nx):
            pass_hidden(k, step)
    for k in range(1, nx):
        finish(k)

    own = pltpu.make_async_copy(ys.at[me], yb.at[place], self_sem.at[1])
    own.start()
    own.wait()
    bytes_of(yb.at[pl.ds(0, ne - 1)], y_recv).wait()
    back = yb[...].reshape(rows, width)
    out_ref[...] = (dot(gate_high, back) + dot(gate_low, back)).astype(BF16)

    bytes_of(mb.at[pl.ds(0, nq - 1)], mk_send).wait()
    for r in range(count):
        bytes_of(tb.at[r, pl.ds(0, nq - 1)], tok_send.at[r]).wait()
        bytes_of(xs.at[r, pl.ds(0, nd - 1)], x_send.at[r]).wait()
    bytes_of(wdt.at[pl.ds(0, nh - 1)], wd_send).wait()
    bytes_of(ys.at[pl.ds(0, ne - 1)], y_send).wait()
    for direction in range(2):
        for k in range(nx):
            for step in range(2):
                ring(direction, step, k).wait_send()
        for k in range(nx):
            for step in range(steps + (1 if antipode(k) == direction else 0)):
                hid(direction, step, k).wait_send()


def local(tokens, expert_ids, gate_scores, gate_weight, up_weight, down_weight):
    ne, nh, ny = lax.axis_size("ep"), lax.axis_size("hs"), CHIPS_Y
    count, model = tokens.shape
    width = model // nh
    part_width = width // CORES
    units = gate_weight.shape[2]
    cap = max(2, 2 * expert_ids.shape[1] * count // ne)
    rows = ne * cap
    nq, nd, nx = ny * CORES, ne // ny, ne // (ny * CORES)
    slices = ((0, 0), (2, -4)) + tuple((i, 0) for i in range(3, nh - 2))
    rounds = len(slices)
    steps = nh // 2 - 1
    dma = pltpu.SemaphoreType.DMA
    hbm = pl.BlockSpec(memory_space=pltpu.MemorySpace.HBM)
    vmem = pl.BlockSpec(memory_space=pltpu.MemorySpace.VMEM)
    return pl.pallas_call(
        functools.partial(kernel, ne, nh, ny, cap, slices, min(2, rounds - 2)),
        out_shape=jax.ShapeDtypeStruct((count, width), BF16),
        in_specs=[hbm, vmem, vmem, hbm, hbm, hbm],
        out_specs=vmem,
        scratch_shapes=[
            pltpu.VMEM((count, model), BF16),
            pltpu.VMEM((ny, nd, 128), F32),
            pltpu.VMEM((nq, nd, 128), F32),
            pltpu.VMEM((rounds, nq, count, part_width), BF16),
            pltpu.VMEM((nd, nq * cap, nq * count), BF16),
            pltpu.VMEM((rounds, nd, nq * cap, part_width), BF16),
            pltpu.VMEM((nh, nx, nq * cap, width), BF16),
            pltpu.VMEM((model, 2 * units), BF16),
            pltpu.VMEM((nh, units, width), BF16),
            pltpu.VMEM((nx, nq * cap, 2 * units), F32),
            pltpu.VMEM((nh, nx, nq * cap, units), BF16),
            pltpu.VMEM((ne, cap, width), BF16),
            pltpu.VMEM((ne, cap, width), BF16),
            pltpu.VMEM((nx, nq * cap, width), F32),
            dma((4,)), dma((rounds,)), dma((2,)), dma, dma, dma((rounds,)), dma((rounds,)),
            dma((rounds,)), dma((rounds, nx)), dma, dma,
            dma((2, 2, nx)), dma((2, 2, nx)),
            dma((2, steps + 1, nx)), dma((2, steps + 1, nx)), dma, dma,
        ],
        compiler_params=pltpu.CompilerParams(
            collective_id=0, has_side_effects=True, vmem_limit_bytes=63 << 20),
    )(tokens, expert_ids.T, gate_scores.T, gate_weight, up_weight, down_weight)


def solution(mesh):
    placed = (
        P("ep", None),
        P("ep", None),
        P("ep", None),
        P("ep", None, "hs"),
        P("ep", None, "hs"),
        P("ep", "hs", None),
    )
    return jax.shard_map(
        local, mesh=mesh, in_specs=placed, out_specs=P("ep", "hs"), check_vma=False
    )
```
